32 devices in a mesh: groups: 2 (over x), kv: 16 (over z, y, core).
Axes of the slice: x: 2, y: 2, z: 4, core: 2. Of those that a mesh axis runs over, the one named last changes fastest.
Arguments:
- queries: bfloat16 [64, 8192], P(('groups', 'kv')), parts along dimension 0, may hold values from -48 to 48
- keys: bfloat16 [16384, 1024], P(('groups', 'kv')), parts along dimension 0, may hold values from -6 to 6
- values: bfloat16 [16384, 1024], P(('groups', 'kv')), parts along dimension 0, may hold values from -6 to 6
- block_live: int32 [32, 128], P('groups', 'kv'), parts along dimension 0, may hold values from 0 to 1, as said below
- span_offset: int32 [2], P('groups'), parts along dimension 0, may hold values from 2048 to 7648
Outputs:
- attended: bfloat16 [64, 8192], P(('groups', 'kv')), parts along dimension 0
The draws below stay inside these ranges and needn't reach their ends.
There are 2 independent parts, one for each index of `groups`. The reference program is written for one: setup_inputs(seed, part) draws one part's arguments, and reference() takes and returns one part's arrays. A program takes and returns all parts, laid end to end along the dimension named above; each array names one. Nothing has to cross between parts.
Inputs may be any that keep to these rules, and one draw needn't show every extreme that they name: `block_live`: column 0 is 1 for every query shard.
All inputs are finite; a program needn't handle non-finite values.
Results may differ from the reference program's by a relative error of at most 0.0018.
Values may be sent and summed in bfloat16 or wider, within the bound.
A program may use at most 128 MiB of HBM per device.

```python
import math
import jax
import jax.numpy as jnp
from jax import lax

H = 64
KVH = 8
HD = 128
BLK = 64
KV_DEV = 512
Q_DEV = 2
GROUP = 8
SEG = 256
CACHE = 8192
Q_TOTAL = 32
QSH = 16
NKB = 128


def draw_keys(key, part):
    cells = jnp.clip(jax.random.normal(jax.random.fold_in(key, 11), (CACHE, KVH * HD), jnp.float32), -6.0, 6.0)
    return cells.astype(jnp.bfloat16)


def draw_queries(key, part):
    cells = 3.0 * jnp.clip(jax.random.normal(jax.random.fold_in(key, 12), (Q_TOTAL, H * HD), jnp.float32), -6.0, 6.0)
    cells = jnp.clip(cells, -48.0, 48.0)
    return cells.astype(jnp.bfloat16)


def draw_block_live(key, part):
    picks = jax.random.randint(jax.random.fold_in(key, 13), (QSH, NKB), 0, 4)
    cells = (picks > 0).astype(jnp.int32)
    return cells.at[:, 0].set(1)


def level_of(key, extent, split, low, high):
    gain, own = 1.0, jax.random.fold_in(key, 6)
    for dim, blocks in split:
        steps = jnp.exp(jax.random.uniform(jax.random.fold_in(own, dim), (blocks,), jnp.float32, low / len(split), high / len(split)))
        gain = gain * jnp.repeat(steps, extent[dim] // blocks).reshape([-1 if axis == dim else 1 for axis in range(len(extent))])
    return gain


def scatter_about(key, shape, spread, most, pieces=(), held_as=jnp.bfloat16):
    drawn = spread * jax.random.normal(key, shape, jnp.float32)
    if pieces:
        drawn = drawn * level_of(key, shape, pieces, -0.22, 0.18)
    return jnp.clip(drawn, -most, most).astype(held_as)


def setup_inputs(seed: int = 0, part: int = 0) -> dict:
    key_list = jax.random.split(jax.random.key(seed), 6)
    own_keys = jax.random.split(jax.random.fold_in(key_list[5], part), 6)
    queries = draw_queries(jax.random.fold_in(jax.random.fold_in(key_list[5], part), 71), part)
    keys = draw_keys(jax.random.fold_in(jax.random.fold_in(key_list[5], part), 71), part)
    values = scatter_about(own_keys[2], (CACHE, KVH * HD), 1.0, 6.0, ((0, 16),))
    block_live = draw_block_live(jax.random.fold_in(jax.random.fold_in(key_list[5], part), 71), part)
    span_offset = jax.random.randint(own_keys[4], (1,), CACHE // 4, CACHE - KV_DEV - Q_TOTAL + 1).astype(jnp.int32)
    return dict(queries=queries, keys=keys, values=values, block_live=block_live, span_offset=span_offset)


SCORE_FLOOR = -30.0

def segment_terms(queries, keys, values, block_live, offset, seg_start):
    queries_four = queries.reshape(Q_TOTAL, KVH, GROUP, HD).astype(jnp.float32)
    key_part = lax.dynamic_slice_in_dim(keys, seg_start, SEG, 0).reshape(SEG, KVH, HD).astype(jnp.float32)
    value_part = lax.dynamic_slice_in_dim(values, seg_start, SEG, 0).reshape(SEG, KVH, HD).astype(jnp.float32)
    scores = jnp.einsum('qgeh,kgh->qgek', queries_four, key_part) * (1.0 / math.sqrt(HD))
    positions = seg_start + jnp.arange(SEG, dtype=jnp.int32)
    queries_at = offset + jnp.arange(Q_TOTAL, dtype=jnp.int32)
    live_cols = lax.dynamic_slice_in_dim(block_live, (seg_start // BLK).astype(jnp.int32), SEG // BLK, 1)
    live_cells = jnp.repeat(jnp.repeat(live_cols, Q_DEV, axis=0), BLK, axis=1) > 0
    allowed = (positions[None, :] <= queries_at[:, None]) & ((positions[None, :] >= offset) | live_cells)
    allowed_four = allowed[:, None, None, :]
    peaks = lax.optimization_barrier(jnp.max(jnp.where(allowed_four, scores, SCORE_FLOOR), axis=3))
    weights = jnp.where(allowed_four, jnp.exp(scores - peaks[..., None]), 0.0)
    totals = lax.optimization_barrier(jnp.sum(weights, axis=3))
    rounded = lax.optimization_barrier(weights.astype(jnp.bfloat16)).astype(jnp.float32)
    partial_out = jnp.einsum('qgek,kgh->qgeh', rounded, value_part)
    return (partial_out.reshape(Q_TOTAL, H * HD), peaks.reshape(Q_TOTAL, H), totals.reshape(Q_TOTAL, H))

def reference(queries, keys, values, block_live, span_offset):
    offset = span_offset[0]
    last_pos = offset + Q_TOTAL - 1

    def nothing(unused):
        return (jnp.zeros((Q_TOTAL, H * HD), jnp.float32), jnp.full((Q_TOTAL, H), SCORE_FLOOR, jnp.float32), jnp.zeros((Q_TOTAL, H), jnp.float32))

    def step(state_now, seg_index):
        weighted, peak_all, total_all = state_now
        seg_start = (seg_index * SEG).astype(jnp.int32)

        def compute(unused):
            return segment_terms(queries, keys, values, block_live, offset, seg_start)
        part_out, part_peak, part_total = lax.cond(seg_start <= last_pos, compute, nothing, 0)
        new_peak = jnp.maximum(peak_all, part_peak)
        old_scale = jnp.exp(peak_all - new_peak)
        new_scale = jnp.exp(part_peak - new_peak)
        weighted = weighted * jnp.repeat(old_scale, HD, axis=1) + part_out * jnp.repeat(new_scale, HD, axis=1)
        total_all = total_all * old_scale + part_total * new_scale
        return ((weighted, new_peak, total_all), 0)
    final_state, unused = lax.scan(step, nothing(0), jnp.arange(CACHE // SEG, dtype=jnp.int32))
    weighted, peak_all, total_all = final_state
    return (weighted / jnp.repeat(total_all, HD, axis=1)).astype(jnp.bfloat16)
```

```python
import functools
import math

import jax
import jax.numpy as jnp
from jax import lax
from jax.experimental import pallas as pl
from jax.experimental.pallas import tpu as pltpu
from jax.sharding import PartitionSpec as P

HD = 128
BLK = 64
SEG = 256
SCORE_FLOOR = -30.0
MASKED = -1e30
STEPS = 32767.0
CHUNKS = 4
STATS = 4
MESH = pl.DeviceIdType.MESH


def flip(index, mask):
    result = index
    bit = 1
    while bit <= mask:
        if mask & bit:
            result = result + bit - 2 * bit * ((index // bit) % 2)
        bit *= 2
    return result


def xor(a, b, n):
    result = 0
    bit = 1
    while bit < n:
        result = result + (a // bit + b // bit) % 2 * bit
        bit *= 2
    return result


def build_bias(n, tile, q_dev, me, holder, kv_dev, live_ref, offset):
    rows = n * tile
    blocks, shards = live_ref.shape
    live = (live_ref[...] > 0).astype(jnp.float32).astype(jnp.bfloat16)
    row = lax.broadcasted_iota(jnp.int32, (rows, shards), 0)
    col = lax.broadcasted_iota(jnp.int32, (rows, shards), 1)
    pick = ((row // tile) ^ me == col).astype(jnp.float32).astype(jnp.bfloat16)
    spread = lax.broadcasted_iota(jnp.int32, (blocks, kv_dev), 1) // BLK
    spread = (spread == lax.broadcasted_iota(jnp.int32, (blocks, kv_dev), 0)).astype(jnp.float32)
    by_row = lax.dot_general(
        pick, live, (((1,), (1,)), ((), ())), preferred_element_type=jnp.float32
    ).astype(jnp.bfloat16)
    cells = jnp.dot(by_row, spread.astype(jnp.bfloat16), preferred_element_type=jnp.float32)
    position = holder * kv_dev + lax.broadcasted_iota(jnp.int32, (1, kv_dev), 1)
    row1 = lax.broadcasted_iota(jnp.int32, (rows, 1), 0)
    at = offset + ((row1 // tile) ^ me) * q_dev + row1 % q_dev
    allowed = (position <= at) & ((position >= offset) | (cells > 0.5))
    return jnp.where(allowed, 0.0, MASKED)


def kernel(
    n, q_dev, offset_ref, live_hbm, q_hbm, k_hbm, v_hbm, out_ref,
    q_ref, live_ref, qbuf, kbuf, vbuf, lbuf, bias, obuf, rbuf, sbuf, sgot, mdiag, tdiag, adiag,
    kv_sem, in_sem, l_send, l_recv, k_send, k_recv, v_send, v_recv,
    q_send, q_recv, o_send, o_recv, s_send, s_recv,
):
    me = lax.axis_index("kv")
    heads, tile, _ = q_hbm.shape
    kv_dev = k_hbm.shape[0]
    half = heads // 2
    per = half // CHUNKS
    wide = per * HD
    rows = n * tile
    far = n // 4
    core = me % 2
    y = me // 2 % 2
    z = me // 4
    mate = 1 - core

    def remote(src, dst, send, recv, slot):
        return pltpu.make_async_remote_copy(
            src_ref=src, dst_ref=dst, send_sem=send, recv_sem=recv,
            device_id={"kv": flip(me, slot)}, device_id_type=MESH,
        )

    def targets(step):
        found = []
        for k in range(1, far):
            to = (z + far + step * k) % far
            base = xor(z, to, far) * 4
            for yd in range(2)[::step]:
                for cd in range(2):
                    slot = base + (y + yd) % 2 * 2 + (core + cd) % 2
                    found.append((slot, to * 4 + yd * 2 + cd, cd))
        for s in (3, 2, 1):
            found.append((s, flip(me, s), core if s % 2 == 0 else mate))
        return found

    def push(src, dst, send, recv, device):
        pltpu.make_async_remote_copy(
            src_ref=src, dst_ref=dst, send_sem=send, recv_sem=recv,
            device_id={"kv": device}, device_id_type=MESH,
        ).start()

    def columns(side, c):
        return pl.ds(pl.multiple_of(side * (half * HD) + c * wide, HD), wide)

    barrier = pltpu.get_barrier_semaphore()
    for s in reversed(range(1, n)):
        pl.semaphore_signal(
            barrier, inc=1, device_id={"kv": flip(me, s)}, device_id_type=MESH
        )
    q_load = pltpu.make_async_copy(q_hbm, q_ref, in_sem.at[0])
    live_load = pltpu.make_async_copy(live_hbm, live_ref, in_sem.at[1])
    q_load.start()
    live_load.start()
    own = pl.ds(0, kv_dev)
    theirs = pl.ds(kv_dev, kv_dev)
    loads = []
    for c in range(CHUNKS):
        here = pl.ds(c * wide, wide)
        k_load = pltpu.make_async_copy(
            k_hbm.at[:, columns(core, c)], kbuf.at[own, here], kv_sem.at[0, c]
        )
        v_load = pltpu.make_async_copy(
            v_hbm.at[:, columns(core, c)], vbuf.at[own, here], kv_sem.at[1, c]
        )
        k_load.start()
        v_load.start()
        loads.append((k_load, v_load))
    q_load.wait()
    pl.semaphore_wait(barrier, n - 1)

    live_copy = remote(live_hbm, lbuf, l_send.at[0], l_recv.at[0], 1)
    swaps = []
    outward = targets(-1)
    for c in range(CHUNKS):
        part = pl.ds(c * per, per)
        for slot, device, side in outward:
            push(
                q_ref.at[pl.ds(side * half + c * per, per)], qbuf.at[part, slot],
                q_send.at[c], q_recv.at[c], device,
            )
    live_copy.start()
    for c in range(CHUNKS):
        here = pl.ds(c * wide, wide)
        k_swap = remote(
            k_hbm.at[:, columns(mate, c)], kbuf.at[theirs, here], k_send.at[c], k_recv.at[c], 1
        )
        v_swap = remote(
            v_hbm.at[:, columns(mate, c)], vbuf.at[theirs, here], v_send.at[c], v_recv.at[c], 1
        )
        k_swap.start()
        v_swap.start()
        swaps.append((k_swap, v_swap))

    live_load.wait()
    qbuf[:, 0] = q_ref[pl.ds(core * half, half)]
    offset = offset_ref[0]
    bias[:, :kv_dev] = build_bias(n, tile, q_dev, me, me, kv_dev, live_ref, offset)
    live_copy.wait()
    bias[:, kv_dev:] = build_bias(n, tile, q_dev, me, flip(me, 1), kv_dev, lbuf, offset)

    inward = targets(1)
    others = pl.ds(1, n - 1)
    score_scale = 1.0 / math.sqrt(HD)
    lane = lax.broadcasted_iota(jnp.int32, (rows, HD), 1)
    row = lax.broadcasted_iota(jnp.int32, (rows, HD), 0) % tile

    for c in range(CHUNKS):
        part = pl.ds(c * per, per)
        for copy in loads[c]:
            copy.wait()
        for copy in swaps[c]:
            copy.wait_recv()
        rest = qbuf.at[part, others]
        pltpu.make_async_copy(rest, rest, q_recv.at[c]).wait()
        for g in range(c * per, (c + 1) * per):
            queries = qbuf[g].reshape(rows, HD)
            cols = slice(g * HD, (g + 1) * HD)
            accs, peaks, totals = [], [], []
            for s in range(2 * kv_dev // SEG):
                keys = slice(s * SEG, (s + 1) * SEG)
                scores = lax.dot_general(
                    queries, kbuf[keys, cols], (((1,), (1,)), ((), ())),
                    preferred_element_type=jnp.float32,
                )
                scores = scores * score_scale + bias[:, keys]
                peak = jnp.maximum(jnp.max(scores, axis=1, keepdims=True), SCORE_FLOOR)
                weights = jnp.exp(scores - peak)
                totals.append(jnp.sum(weights, axis=1, keepdims=True))
                peaks.append(peak)
                accs.append(
                    jnp.dot(
                        weights.astype(jnp.bfloat16), vbuf[keys, cols],
                        preferred_element_type=jnp.float32,
                    )
                )
            peak = functools.reduce(jnp.maximum, peaks)
            scales = [jnp.exp(p - peak) for p in peaks]
            acc = sum(a * e for a, e in zip(accs, scales))
            total = sum(t * e for t, e in zip(totals, scales))
            most = jnp.max(jnp.abs(acc), axis=1, keepdims=True)
            inverse = jnp.where(most > 0.0, 1.0 / most, 0.0)
            coded = jnp.round(acc * inverse * STEPS).astype(jnp.int32).astype(jnp.int16)
            obuf[g] = coded.reshape(n, tile, HD)
            here = lane == g * tile + row
            if g == 0:
                mdiag[...] = jnp.where(here, peak, 0.0)
                tdiag[...] = jnp.where(here, total, 0.0)
                adiag[...] = jnp.where(here, most, 0.0)
            else:
                mdiag[...] = jnp.where(here, peak, mdiag[...])
                tdiag[...] = jnp.where(here, total, tdiag[...])
                adiag[...] = jnp.where(here, most, adiag[...])
        if c == CHUNKS - 1:
            for k, diag in enumerate((mdiag, tdiag, adiag)):
                for s in range(n):
                    line = jnp.sum(diag[s * tile : (s + 1) * tile], axis=0, keepdims=True)
                    if s == 0:
                        sgot[0, 0, k : k + 1] = line
                    else:
                        sbuf[s, k : k + 1] = line
            for slot, device, _ in inward:
                push(
                    sbuf.at[slot], sgot.at[slot // 2, slot % 2], s_send.at[0], s_recv.at[0], device
                )
        for slot, device, _ in inward:
            push(obuf.at[part, slot], rbuf.at[part, slot], o_send.at[c], o_recv.at[c], device)

    stats_in = sbuf.at[others]
    pltpu.make_async_copy(stats_in, stats_in, s_recv.at[0]).wait()
    weight = []
    for a in range(2):
        peaks = sgot[:, a, 0]
        peak = jnp.max(peaks, axis=0, keepdims=True)
        scale = jnp.exp(peaks - peak)
        total = jnp.sum(scale * sgot[:, a, 1], axis=0, keepdims=True)
        weight.append(jnp.transpose(scale * (sgot[:, a, 2] / total)))
    for c in range(CHUNKS):
        part = pl.ds(c * per, per)
        rest = rbuf.at[part, others]
        pltpu.make_async_copy(rest, rest, o_recv.at[c]).wait()
        for g in range(c * per, (c + 1) * per):
            span = slice(g * tile, (g + 1) * tile)
            for a in range(2):
                acc = None
                for chip in range(n // 2):
                    s = chip * 2 + a
                    block = obuf[g, 0] if s == 0 else rbuf[g, s]
                    term = block.astype(jnp.int32).astype(jnp.float32)
                    term = term * weight[a][span, chip : chip + 1]
                    acc = term if acc is None else acc + term
                side = core if a == 0 else mate
                out_ref[side * half + g] = (acc * (1.0 / STEPS)).astype(jnp.bfloat16)

    for c in range(CHUNKS):
        part = pl.ds(c * per, per)
        rest = qbuf.at[part, others]
        pltpu.make_async_copy(rest, rest, q_send.at[c]).wait()
        for copy in swaps[c]:
            copy.wait_send()
        rest = obuf.at[part, others]
        pltpu.make_async_copy(rest, rest, o_send.at[c]).wait()
    pltpu.make_async_copy(stats_in, stats_in, s_send.at[0]).wait()


def on_device(queries, keys, values, block_live, span_offset):
    n = lax.axis_size("kv")
    q_dev, width = queries.shape
    kv_dev, kv_width = keys.shape
    shards, blocks = block_live.shape
    heads = kv_width // HD
    half = heads // 2
    group = width // kv_width
    tile = group * q_dev
    rows = n * tile
    tiles = queries.reshape(q_dev, heads * group, HD).transpose(1, 0, 2).reshape(heads, tile, HD)
    vmem = pl.BlockSpec(memory_space=pltpu.VMEM)
    hbm = pl.BlockSpec(memory_space=pltpu.HBM)
    dma = pltpu.SemaphoreType.DMA
    out = pl.pallas_call(
        functools.partial(kernel, n, q_dev),
        out_shape=jax.ShapeDtypeStruct((heads, tile, HD), jnp.bfloat16),
        in_specs=[pl.BlockSpec(memory_space=pltpu.SMEM), hbm, hbm, hbm, hbm],
        out_specs=vmem,
        scratch_shapes=[
            pltpu.VMEM((heads, tile, HD), jnp.bfloat16),
            pltpu.VMEM((blocks, shards), jnp.int32),
            pltpu.VMEM((half, n, tile, HD), jnp.bfloat16),
            pltpu.VMEM((2 * kv_dev, kv_width // 2), jnp.bfloat16),
            pltpu.VMEM((2 * kv_dev, kv_width // 2), jnp.bfloat16),
            pltpu.VMEM((blocks, shards), jnp.int32),
            pltpu.VMEM((rows, 2 * kv_dev), jnp.float32),
            pltpu.VMEM((half, n, tile, HD), jnp.int16),
            pltpu.VMEM((half, n, tile, HD), jnp.int16),
            pltpu.VMEM((n, STATS, HD), jnp.float32),
            pltpu.VMEM((n // 2, 2, STATS, HD), jnp.float32),
            pltpu.VMEM((rows, HD), jnp.float32),
            pltpu.VMEM((rows, HD), jnp.float32),
            pltpu.VMEM((rows, HD), jnp.float32),
            dma((2, CHUNKS)), dma((2,)), dma((1,)), dma((1,)),
            *[dma((CHUNKS,)) for _ in range(8)],
            dma((1,)), dma((1,)),
        ],
        compiler_params=pltpu.CompilerParams(
            collective_id=0, has_side_effects=True, vmem_limit_bytes=53 * 1024 * 1024
        ),
    )(span_offset, *(pltpu.with_memory_space_constraint(x, pltpu.HBM) for x in (block_live.T, tiles, keys, values)))
    return out.reshape(heads * group, q_dev, HD).transpose(1, 0, 2).reshape(q_dev, width)


def solution(mesh):
    placed = (
        P(("groups", "kv"), None),
        P(("groups", "kv"), None),
        P(("groups", "kv"), None),
        P("groups", "kv"),
        P("groups"),
    )
    return jax.shard_map(
        on_device, mesh=mesh, in_specs=placed, out_specs=P(("groups", "kv"), None), check_vma=False
    )
```

```python
import functools
import math

import jax
import jax.numpy as jnp
from jax import lax
from jax.experimental import pallas as pl
from jax.experimental.pallas import tpu as pltpu
from jax.sharding import PartitionSpec as P

HD = 128
BLK = 64
LOG2E = math.log2(math.e)
SCORE_FLOOR = -30.0
MASKED = -1e30
STEPS = 32767.0
CHUNKS = 2
SPLIT = 1
MESH = pl.DeviceIdType.MESH


def flip(index, mask):
    result = index
    bit = 1
    while bit <= mask:
        if mask & bit:
            result = result + bit - 2 * bit * ((index // bit) % 2)
        bit *= 2
    return result


def xor(a, b, n):
    result = 0
    bit = 1
    while bit < n:
        result = result + (a // bit + b // bit) % 2 * bit
        bit *= 2
    return result


def build_bias(n, tile, q_dev, me, holder, kv_dev, live_ref, offset):
    rows = n * tile
    blocks, shards = live_ref.shape
    live = (live_ref[...] > 0).astype(jnp.float32).astype(jnp.bfloat16)
    row = lax.broadcasted_iota(jnp.int32, (rows, shards), 0)
    col = lax.broadcasted_iota(jnp.int32, (rows, shards), 1)
    pick = ((row // tile) ^ me == col).astype(jnp.float32).astype(jnp.bfloat16)
    spread = lax.broadcasted_iota(jnp.int32, (blocks, kv_dev), 1) // BLK
    spread = (spread == lax.broadcasted_iota(jnp.int32, (blocks, kv_dev), 0)).astype(jnp.float32)
    by_row = lax.dot_general(
        pick, live, (((1,), (1,)), ((), ())), preferred_element_type=jnp.float32
    ).astype(jnp.bfloat16)
    cells = jnp.dot(by_row, spread.astype(jnp.bfloat16), preferred_element_type=jnp.float32)
    position = holder * kv_dev + lax.broadcasted_iota(jnp.int32, (1, kv_dev), 1)
    row1 = lax.broadcasted_iota(jnp.int32, (rows, 1), 0)
    at = offset + ((row1 // tile) ^ me) * q_dev + row1 % q_dev
    allowed = (position <= at) & ((position >= offset) | (cells > 0.5))
    return jnp.where(allowed, 0.0, MASKED)


def kernel(
    n, q_dev, offset_ref, live_hbm, q_hbm, k_hbm, v_hbm, out_ref,
    q_ref, live_ref, qbuf, kbuf, vbuf, lbuf, bias, obuf, rbuf, sbuf, sgot, diag,
    kv_sem, in_sem, l_send, l_recv, k_send, k_recv, v_send, v_recv,
    q_send, q_recv, o_send, o_recv, s_send, s_recv,
):
    me = lax.axis_index("kv")
    heads, tile, _ = q_hbm.shape
    kv_dev = k_hbm.shape[0]
    half = heads // 2
    per = half // CHUNKS
    wide = per * HD
    rows = n * tile
    far = n // 4
    core = me % 2
    y = me // 2 % 2
    z = me // 4
    mate = 1 - core

    def remote(src, dst, send, recv, slot):
        return pltpu.make_async_remote_copy(
            src_ref=src, dst_ref=dst, send_sem=send, recv_sem=recv,
            device_id={"kv": flip(me, slot)}, device_id_type=MESH,
        )

    def targets(step):
        found = []
        for k in range(1, far):
            to = (z + far + step * k) % far
            base = xor(z, to, far) * 4
            for yd in range(2)[::step]:
                for cd in range(2):
                    slot = base + (y + yd) % 2 * 2 + (core + cd) % 2
                    found.append((slot, to * 4 + yd * 2 + cd, cd))
        for s in (3, 2, 1):
            found.append((s, flip(me, s), core if s % 2 == 0 else mate))
        return found

    def push(src, dst, send, recv, device):
        pltpu.make_async_remote_copy(
            src_ref=src, dst_ref=dst, send_sem=send, recv_sem=recv,
            device_id={"kv": device}, device_id_type=MESH,
        ).start()

    def columns(side, c):
        return pl.ds(pl.multiple_of(side * (half * HD) + c * wide, HD), wide)

    barrier = pltpu.get_barrier_semaphore()
    for s in reversed(range(1, n)):
        pl.semaphore_signal(
            barrier, inc=1, device_id={"kv": flip(me, s)}, device_id_type=MESH
        )
    q_load = pltpu.make_async_copy(q_hbm, q_ref, in_sem.at[0])
    live_load = pltpu.make_async_copy(live_hbm, live_ref, in_sem.at[1])
    q_load.start()
    live_load.start()
    own = pl.ds(0, kv_dev)
    theirs = pl.ds(kv_dev, kv_dev)
    loads = []
    for c in range(CHUNKS):
        here = pl.ds(c * wide, wide)
        k_load = pltpu.make_async_copy(
            k_hbm.at[:, columns(core, c)], kbuf.at[own, here], kv_sem.at[0, c]
        )
        v_load = pltpu.make_async_copy(
            v_hbm.at[:, columns(core, c)], vbuf.at[own, here], kv_sem.at[1, c]
        )
        k_load.start()
        v_load.start()
        loads.append((k_load, v_load))
    q_load.wait()
    pl.semaphore_wait(barrier, n - 1)

    live_copy = remote(live_hbm, lbuf, l_send.at[0], l_recv.at[0], 1)
    swaps = []
    outward = targets(-1)
    for c in range(CHUNKS):
        part = pl.ds(c * per, per)
        for slot, device, side in outward:
            push(
                q_ref.at[pl.ds(side * half + c * per, per)], qbuf.at[part, slot],
                q_send.at[c], q_recv.at[c], device,
            )
    live_copy.start()
    for c in range(CHUNKS):
        here = pl.ds(c * wide, wide)
        k_swap = remote(
            k_hbm.at[:, columns(mate, c)], kbuf.at[theirs, here], k_send.at[c], k_recv.at[c], 1
        )
        v_swap = remote(
            v_hbm.at[:, columns(mate, c)], vbuf.at[theirs, here], v_send.at[c], v_recv.at[c], 1
        )
        k_swap.start()
        v_swap.start()
        swaps.append((k_swap, v_swap))

    live_load.wait()
    qbuf[:, 0] = q_ref[pl.ds(core * half, half)]
    offset = offset_ref[0]
    bias[:, :kv_dev] = build_bias(n, tile, q_dev, me, me, kv_dev, live_ref, offset)
    live_copy.wait()
    bias[:, kv_dev:] = build_bias(n, tile, q_dev, me, flip(me, 1), kv_dev, lbuf, offset)

    inward = targets(1)
    others = pl.ds(1, n - 1)
    score_scale = LOG2E / math.sqrt(HD)
    strip = rows // SPLIT
    lane = lax.broadcasted_iota(jnp.int32, (strip, HD), 1)
    row = lax.broadcasted_iota(jnp.int32, (strip, HD), 0) % tile

    for c in range(CHUNKS):
        part = pl.ds(c * per, per)
        for copy in loads[c]:
            copy.wait()
        for copy in swaps[c]:
            copy.wait_recv()
        rest = qbuf.at[part, others]
        pltpu.make_async_copy(rest, rest, q_recv.at[c]).wait()
        for g in range(c * per, (c + 1) * per):
            cols = slice(g * HD, (g + 1) * HD)
            for r in range(SPLIT):
                mine = slice(r * strip, (r + 1) * strip)
                slots = slice(r * n // SPLIT, (r + 1) * n // SPLIT)
                queries = qbuf[g, slots].reshape(strip, HD)
                scores = lax.dot_general(
                    queries, kbuf[:, cols], (((1,), (1,)), ((), ())),
                    preferred_element_type=jnp.float32,
                )
                scores = scores * score_scale + bias[mine]
                peak = jnp.max(scores, axis=1, keepdims=True)
                peak = jnp.maximum(peak, SCORE_FLOOR * LOG2E)
                weights = jnp.exp2(scores - peak)
                total = jnp.sum(weights, axis=1, keepdims=True)
                acc = jnp.dot(
                    weights.astype(jnp.bfloat16), vbuf[:, cols],
                    preferred_element_type=jnp.float32,
                )
                most = jnp.max(jnp.abs(acc), axis=1, keepdims=True)
                inverse = jnp.where(most > 0.0, STEPS / most, 0.0)
                coded = jnp.round(acc * inverse).astype(jnp.int32).astype(jnp.int16)
                obuf[g, slots] = coded.reshape(n // SPLIT, tile, HD)
                some = total > 0.0
                level = jnp.where(some, peak + jnp.log2(total), MASKED)
                ratio = jnp.where(some, most / total, 0.0)
                before = 0.0 if g == 0 else diag[mine]
                here = lane == g * tile + row
                there = lane == HD // 2 + g * tile + row
                diag[mine] = jnp.where(here, level, jnp.where(there, ratio, before))
        if c == CHUNKS - 1:
            for s in range(n):
                line = jnp.sum(diag[s * tile : (s + 1) * tile], axis=0, keepdims=True)
                if s == 0:
                    sgot[0, 0] = line
                else:
                    sbuf[s] = line
            for slot, device, _ in inward:
                push(
                    sbuf.at[slot], sgot.at[slot // 2, slot % 2], s_send.at[0], s_recv.at[0], device
                )
        for slot, device, _ in inward:
            push(obuf.at[part, slot], rbuf.at[part, slot], o_send.at[c], o_recv.at[c], device)

    stats_in = sbuf.at[others]
    pltpu.make_async_copy(stats_in, stats_in, s_recv.at[0]).wait()
    weight = []
    for a in range(2):
        levels = sgot[:, a, 0]
        ratios = pltpu.roll(levels, HD // 2, 1)
        scale = jnp.exp2(levels - jnp.max(levels, axis=0, keepdims=True))
        total = jnp.sum(scale, axis=0, keepdims=True)
        weight.append(jnp.transpose(scale * (ratios / total)))
    for c in range(CHUNKS):
        part = pl.ds(c * per, per)
        rest = rbuf.at[part, others]
        pltpu.make_async_copy(rest, rest, o_recv.at[c]).wait()
        for g in range(c * per, (c + 1) * per):
            span = slice(g * tile, (g + 1) * tile)
            for a in range(2):
                acc = None
                for chip in range(n // 2):
                    s = chip * 2 + a
                    block = obuf[g, 0] if s == 0 else rbuf[g, s]
                    term = block.astype(jnp.int32).astype(jnp.float32)
                    term = term * weight[a][span, chip : chip + 1]
                    acc = term if acc is None else acc + term
                side = core if a == 0 else mate
                out_ref[side * half + g] = (acc * (1.0 / STEPS)).astype(jnp.bfloat16)

    for c in range(CHUNKS):
        part = pl.ds(c * per, per)
        rest = qbuf.at[part, others]
        pltpu.make_async_copy(rest, rest, q_send.at[c]).wait()
        for copy in swaps[c]:
            copy.wait_send()
        rest = obuf.at[part, others]
        pltpu.make_async_copy(rest, rest, o_send.at[c]).wait()
    pltpu.make_async_copy(stats_in, stats_in, s_send.at[0]).wait()


def on_device(queries, keys, values, block_live, span_offset):
    n = lax.axis_size("kv")
    q_dev, width = queries.shape
    kv_dev, kv_width = keys.shape
    shards, blocks = block_live.shape
    heads = kv_width // HD
    half = heads // 2
    group = width // kv_width
    tile = group * q_dev
    rows = n * tile
    assert half * tile <= HD // 2
    tiles = queries.reshape(q_dev, heads * group, HD).transpose(1, 0, 2).reshape(heads, tile, HD)
    vmem = pl.BlockSpec(memory_space=pltpu.VMEM)
    hbm = pl.BlockSpec(memory_space=pltpu.HBM)
    dma = pltpu.SemaphoreType.DMA
    out = pl.pallas_call(
        functools.partial(kernel, n, q_dev),
        out_shape=jax.ShapeDtypeStruct((heads, tile, HD), jnp.bfloat16),
        in_specs=[pl.BlockSpec(memory_space=pltpu.SMEM), hbm, hbm, hbm, hbm],
        out_specs=vmem,
        scratch_shapes=[
            pltpu.VMEM((heads, tile, HD), jnp.bfloat16),
            pltpu.VMEM((blocks, shards), jnp.int32),
            pltpu.VMEM((half, n, tile, HD), jnp.bfloat16),
            pltpu.VMEM((2 * kv_dev, kv_width // 2), jnp.bfloat16),
            pltpu.VMEM((2 * kv_dev, kv_width // 2), jnp.bfloat16),
            pltpu.VMEM((blocks, shards), jnp.int32),
            pltpu.VMEM((rows, 2 * kv_dev), jnp.float32),
            pltpu.VMEM((half, n, tile, HD), jnp.int16),
            pltpu.VMEM((half, n, tile, HD), jnp.int16),
            pltpu.VMEM((n, 1, HD), jnp.float32),
            pltpu.VMEM((n // 2, 2, 1, HD), jnp.float32),
            pltpu.VMEM((rows, HD), jnp.float32),
            dma((2, CHUNKS)), dma((2,)), dma((1,)), dma((1,)),
            *[dma((CHUNKS,)) for _ in range(8)],
            dma((1,)), dma((1,)),
        ],
        compiler_params=pltpu.CompilerParams(
            collective_id=0, has_side_effects=True, vmem_limit_bytes=53 * 1024 * 1024
        ),
    )(span_offset, *(pltpu.with_memory_space_constraint(x, pltpu.HBM) for x in (block_live.T, tiles, keys, values)))
    return out.reshape(heads * group, q_dev, HD).transpose(1, 0, 2).reshape(q_dev, width)


def solution(mesh):
    placed = (
        P(("groups", "kv"), None),
        P(("groups", "kv"), None),
        P(("groups", "kv"), None),
        P("groups", "kv"),
        P("groups"),
    )
    return jax.shard_map(
        on_device, mesh=mesh, in_specs=placed, out_specs=P(("groups", "kv"), None), check_vma=False
    )
```

```python
import functools
import math

import jax
import jax.numpy as jnp
from jax import lax
from jax.experimental import pallas as pl
from jax.experimental.pallas import tpu as pltpu
from jax.sharding import PartitionSpec as P

HD = 128
BLK = 64
SEG = 256
LOG2E = math.log2(math.e)
SCORE_FLOOR = -30.0
MASKED = -1e30
STEPS = 32767.0
CHUNKS = 2
SPLIT = 1
MESH = pl.DeviceIdType.MESH


def flip(index, mask):
    result = index
    bit = 1
    while bit <= mask:
        if mask & bit:
            result = result + bit - 2 * bit * ((index // bit) % 2)
        bit *= 2
    return result


def xor(a, b, n):
    result = 0
    bit = 1
    while bit < n:
        result = result + (a // bit + b // bit) % 2 * bit
        bit *= 2
    return result


def build_bias(n, tile, q_dev, me, holder, kv_dev, live_ref, offset):
    rows = n * tile
    blocks, shards = live_ref.shape
    live = (live_ref[...] > 0).astype(jnp.float32).astype(jnp.bfloat16)
    row = lax.broadcasted_iota(jnp.int32, (rows, shards), 0)
    col = lax.broadcasted_iota(jnp.int32, (rows, shards), 1)
    pick = ((row // tile) ^ me == col).astype(jnp.float32).astype(jnp.bfloat16)
    spread = lax.broadcasted_iota(jnp.int32, (blocks, kv_dev), 1) // BLK
    spread = (spread == lax.broadcasted_iota(jnp.int32, (blocks, kv_dev), 0)).astype(jnp.float32)
    by_row = lax.dot_general(
        pick, live, (((1,), (1,)), ((), ())), preferred_element_type=jnp.float32
    ).astype(jnp.bfloat16)
    cells = jnp.dot(by_row, spread.astype(jnp.bfloat16), preferred_element_type=jnp.float32)
    position = holder * kv_dev + lax.broadcasted_iota(jnp.int32, (1, kv_dev), 1)
    row1 = lax.broadcasted_iota(jnp.int32, (rows, 1), 0)
    at = offset + ((row1 // tile) ^ me) * q_dev + row1 % q_dev
    allowed = (position <= at) & ((position >= offset) | (cells > 0.5))
    return jnp.where(allowed, 0.0, MASKED)


def kernel(
    n, q_dev, offset_ref, live_hbm, q_hbm, k_hbm, v_hbm, out_ref,
    q_ref, live_ref, qbuf, kbuf, vbuf, lbuf, bias, obuf, rbuf, sbuf, sgot, diag,
    kv_sem, in_sem, l_send, l_recv, k_send, k_recv, v_send, v_recv,
    q_send, q_recv, o_send, o_recv, s_send, s_recv,
):
    me = lax.axis_index("kv")
    heads, tile, _ = q_hbm.shape
    kv_dev = k_hbm.shape[0]
    half = heads // 2
    per = half // CHUNKS
    wide = per * HD
    rows = n * tile
    far = n // 4
    core = me % 2
    y = me // 2 % 2
    z = me // 4
    mate = 1 - core

    def remote(src, dst, send, recv, slot):
        return pltpu.make_async_remote_copy(
            src_ref=src, dst_ref=dst, send_sem=send, recv_sem=recv,
            device_id={"kv": flip(me, slot)}, device_id_type=MESH,
        )

    def targets(step):
        found = []
        for k in range(1, far):
            to = (z + far + step * k) % far
            base = xor(z, to, far) * 4
            for yd in range(2)[::step]:
                for cd in range(2):
                    slot = base + (y + yd) % 2 * 2 + (core + cd) % 2
                    found.append((slot, to * 4 + yd * 2 + cd, cd))
        for s in (3, 2, 1):
            found.append((s, flip(me, s), core if s % 2 == 0 else mate))
        return found

    def push(src, dst, send, recv, device):
        pltpu.make_async_remote_copy(
            src_ref=src, dst_ref=dst, send_sem=send, recv_sem=recv,
            device_id={"kv": device}, device_id_type=MESH,
        ).start()

    def columns(side, c):
        return pl.ds(pl.multiple_of(side * (half * HD) + c * wide, HD), wide)

    barrier = pltpu.get_barrier_semaphore()
    for s in reversed(range(1, n)):
        pl.semaphore_signal(
            barrier, inc=1, device_id={"kv": flip(me, s)}, device_id_type=MESH
        )
    q_load = pltpu.make_async_copy(q_hbm, q_ref, in_sem.at[0])
    live_load = pltpu.make_async_copy(live_hbm, live_ref, in_sem.at[1])
    q_load.start()
    live_load.start()
    own = pl.ds(0, kv_dev)
    theirs = pl.ds(kv_dev, kv_dev)
    loads = []
    for c in range(CHUNKS):
        here = pl.ds(c * wide, wide)
        k_load = pltpu.make_async_copy(
            k_hbm.at[:, columns(core, c)], kbuf.at[own, here], kv_sem.at[0, c]
        )
        v_load = pltpu.make_async_copy(
            v_hbm.at[:, columns(core, c)], vbuf.at[own, here], kv_sem.at[1, c]
        )
        k_load.start()
        v_load.start()
        loads.append((k_load, v_load))
    q_load.wait()
    pl.semaphore_wait(barrier, n - 1)

    live_copy = remote(live_hbm, lbuf, l_send.at[0], l_recv.at[0], 1)
    swaps = []
    outward = targets(-1)
    for c in range(CHUNKS):
        part = pl.ds(c * per, per)
        for slot, device, side in outward:
            push(
                q_ref.at[pl.ds(side * half + c * per, per)], qbuf.at[part, slot],
                q_send.at[c], q_recv.at[c], device,
            )
    live_copy.start()
    for c in range(CHUNKS):
        here = pl.ds(c * wide, wide)
        k_swap = remote(
            k_hbm.at[:, columns(mate, c)], kbuf.at[theirs, here], k_send.at[c], k_recv.at[c], 1
        )
        v_swap = remote(
            v_hbm.at[:, columns(mate, c)], vbuf.at[theirs, here], v_send.at[c], v_recv.at[c], 1
        )
        k_swap.start()
        v_swap.start()
        swaps.append((k_swap, v_swap))

    live_load.wait()
    qbuf[:, 0] = q_ref[pl.ds(core * half, half)]
    offset = offset_ref[0]
    bias[:, :kv_dev] = build_bias(n, tile, q_dev, me, me, kv_dev, live_ref, offset)
    live_copy.wait()
    bias[:, kv_dev:] = build_bias(n, tile, q_dev, me, flip(me, 1), kv_dev, lbuf, offset)

    inward = targets(1)
    others = pl.ds(1, n - 1)
    score_scale = LOG2E / math.sqrt(HD)
    strip = rows // SPLIT
    lane = lax.broadcasted_iota(jnp.int32, (strip, HD), 1)
    row = lax.broadcasted_iota(jnp.int32, (strip, HD), 0) % tile

    for c in range(CHUNKS):
        part = pl.ds(c * per, per)
        for copy in loads[c]:
            copy.wait()
        for copy in swaps[c]:
            copy.wait_recv()
        rest = qbuf.at[part, others]
        pltpu.make_async_copy(rest, rest, q_recv.at[c]).wait()
        for g in range(c * per, (c + 1) * per):
            cols = slice(g * HD, (g + 1) * HD)
            for r in range(SPLIT):
                mine = slice(r * strip, (r + 1) * strip)
                slots = slice(r * n // SPLIT, (r + 1) * n // SPLIT)
                queries = qbuf[g, slots].reshape(strip, HD)
                accs, peaks, totals = [], [], []
                for seg in range(2 * kv_dev // SEG):
                    keys = slice(seg * SEG, (seg + 1) * SEG)
                    scores = lax.dot_general(
                        queries, kbuf[keys, cols], (((1,), (1,)), ((), ())),
                        preferred_element_type=jnp.float32,
                    )
                    scores = scores * score_scale + bias[mine, keys]
                    peak = jnp.max(scores, axis=1, keepdims=True)
                    peak = jnp.maximum(peak, SCORE_FLOOR * LOG2E)
                    weights = jnp.exp2(scores - peak)
                    totals.append(jnp.sum(weights, axis=1, keepdims=True))
                    peaks.append(peak)
                    accs.append(
                        jnp.dot(
                            weights.astype(jnp.bfloat16), vbuf[keys, cols],
                            preferred_element_type=jnp.float32,
                        )
                    )
                peak = functools.reduce(jnp.maximum, peaks)
                scales = [jnp.exp2(p - peak) for p in peaks]
                acc = sum(a * e for a, e in zip(accs, scales))
                total = sum(t * e for t, e in zip(totals, scales))
                most = jnp.max(jnp.abs(acc), axis=1, keepdims=True)
                inverse = jnp.where(most > 0.0, STEPS / most, 0.0)
                coded = jnp.round(acc * inverse).astype(jnp.int32).astype(jnp.int16)
                obuf[g, slots] = coded.reshape(n // SPLIT, tile, HD)
                some = total > 0.0
                level = jnp.where(some, peak + jnp.log2(total), MASKED)
                ratio = jnp.where(some, most / total, 0.0)
                before = 0.0 if g == 0 else diag[mine]
                here = lane == g * tile + row
                there = lane == HD // 2 + g * tile + row
                diag[mine] = jnp.where(here, level, jnp.where(there, ratio, before))
        if c == CHUNKS - 1:
            for s in range(n):
                line = jnp.sum(diag[s * tile : (s + 1) * tile], axis=0, keepdims=True)
                if s == 0:
                    sgot[0, 0] = line
                else:
                    sbuf[s] = line
            for slot, device, _ in inward:
                push(
                    sbuf.at[slot], sgot.at[slot // 2, slot % 2], s_send.at[0], s_recv.at[0], device
                )
        for slot, device, _ in inward:
            push(obuf.at[part, slot], rbuf.at[part, slot], o_send.at[c], o_recv.at[c], device)

    stats_in = sbuf.at[others]
    pltpu.make_async_copy(stats_in, stats_in, s_recv.at[0]).wait()
    weight = []
    for a in range(2):
        levels = sgot[:, a, 0]
        ratios = pltpu.roll(levels, HD // 2, 1)
        scale = jnp.exp2(levels - jnp.max(levels, axis=0, keepdims=True))
        total = jnp.sum(scale, axis=0, keepdims=True)
        weight.append(jnp.transpose(scale * (ratios / total)))
    for c in range(CHUNKS):
        part = pl.ds(c * per, per)
        rest = rbuf.at[part, others]
        pltpu.make_async_copy(rest, rest, o_recv.at[c]).wait()
        for g in range(c * per, (c + 1) * per):
            span = slice(g * tile, (g + 1) * tile)
            for a in range(2):
                acc = None
                for chip in range(n // 2):
                    s = chip * 2 + a
                    block = obuf[g, 0] if s == 0 else rbuf[g, s]
                    term = block.astype(jnp.int32).astype(jnp.float32)
                    term = term * weight[a][span, chip : chip + 1]
                    acc = term if acc is None else acc + term
                side = core if a == 0 else mate
                out_ref[side * half + g] = (acc * (1.0 / STEPS)).astype(jnp.bfloat16)

    for c in range(CHUNKS):
        part = pl.ds(c * per, per)
        rest = qbuf.at[part, others]
        pltpu.make_async_copy(rest, rest, q_send.at[c]).wait()
        for copy in swaps[c]:
            copy.wait_send()
        rest = obuf.at[part, others]
        pltpu.make_async_copy(rest, rest, o_send.at[c]).wait()
    pltpu.make_async_copy(stats_in, stats_in, s_send.at[0]).wait()


def on_device(queries, keys, values, block_live, span_offset):
    n = lax.axis_size("kv")
    q_dev, width = queries.shape
    kv_dev, kv_width = keys.shape
    shards, blocks = block_live.shape
    heads = kv_width // HD
    half = heads // 2
    group = width // kv_width
    tile = group * q_dev
    rows = n * tile
    assert half * tile <= HD // 2
    tiles = queries.reshape(q_dev, heads * group, HD).transpose(1, 0, 2).reshape(heads, tile, HD)
    vmem = pl.BlockSpec(memory_space=pltpu.VMEM)
    hbm = pl.BlockSpec(memory_space=pltpu.HBM)
    dma = pltpu.SemaphoreType.DMA
    out = pl.pallas_call(
        functools.partial(kernel, n, q_dev),
        out_shape=jax.ShapeDtypeStruct((heads, tile, HD), jnp.bfloat16),
        in_specs=[pl.BlockSpec(memory_space=pltpu.SMEM), hbm, hbm, hbm, hbm],
        out_specs=vmem,
        scratch_shapes=[
            pltpu.VMEM((heads, tile, HD), jnp.bfloat16),
            pltpu.VMEM((blocks, shards), jnp.int32),
            pltpu.VMEM((half, n, tile, HD), jnp.bfloat16),
            pltpu.VMEM((2 * kv_dev, kv_width // 2), jnp.bfloat16),
            pltpu.VMEM((2 * kv_dev, kv_width // 2), jnp.bfloat16),
            pltpu.VMEM((blocks, shards), jnp.int32),
            pltpu.VMEM((rows, 2 * kv_dev), jnp.float32),
            pltpu.VMEM((half, n, tile, HD), jnp.int16),
            pltpu.VMEM((half, n, tile, HD), jnp.int16),
            pltpu.VMEM((n, 1, HD), jnp.float32),
            pltpu.VMEM((n // 2, 2, 1, HD), jnp.float32),
            pltpu.VMEM((rows, HD), jnp.float32),
            dma((2, CHUNKS)), dma((2,)), dma((1,)), dma((1,)),
            *[dma((CHUNKS,)) for _ in range(8)],
            dma((1,)), dma((1,)),
        ],
        compiler_params=pltpu.CompilerParams(
            collective_id=0, has_side_effects=True, vmem_limit_bytes=53 * 1024 * 1024
        ),
    )(span_offset, *(pltpu.with_memory_space_constraint(x, pltpu.HBM) for x in (block_live.T, tiles, keys, values)))
    return out.reshape(heads * group, q_dev, HD).transpose(1, 0, 2).reshape(q_dev, width)


def solution(mesh):
    placed = (
        P(("groups", "kv"), None),
        P(("groups", "kv"), None),
        P(("groups", "kv"), None),
        P("groups", "kv"),
        P("groups"),
    )
    return jax.shard_map(
        on_device, mesh=mesh, in_specs=placed, out_specs=P(("groups", "kv"), None), check_vma=False
    )
```

```python
import functools
import math

import jax
import jax.numpy as jnp
from jax import lax
from jax.experimental import pallas as pl
from jax.experimental.pallas import tpu as pltpu
from jax.sharding import PartitionSpec as P

HD = 128
BLK = 64
SEG = 256
LOG2E = math.log2(math.e)
SCORE_FLOOR = -30.0
MASKED = -1e30
STEPS = 32767.0
CHUNKS = 2
SPLIT = 1
MESH = pl.DeviceIdType.MESH


def flip(index, mask):
    result = index
    bit = 1
    while bit <= mask:
        if mask & bit:
            result = result + bit - 2 * bit * ((index // bit) % 2)
        bit *= 2
    return result


def xor(a, b, n):
    result = 0
    bit = 1
    while bit < n:
        result = result + (a // bit + b // bit) % 2 * bit
        bit *= 2
    return result


def build_bias(n, tile, q_dev, me, holder, kv_dev, live_ref, offset):
    rows = n * tile
    blocks, shards = live_ref.shape
    live = (live_ref[...] > 0).astype(jnp.float32).astype(jnp.bfloat16)
    row = lax.broadcasted_iota(jnp.int32, (rows, shards), 0)
    col = lax.broadcasted_iota(jnp.int32, (rows, shards), 1)
    pick = ((row // tile) ^ me == col).astype(jnp.float32).astype(jnp.bfloat16)
    spread = lax.broadcasted_iota(jnp.int32, (blocks, kv_dev), 1) // BLK
    spread = (spread == lax.broadcasted_iota(jnp.int32, (blocks, kv_dev), 0)).astype(jnp.float32)
    by_row = lax.dot_general(
        pick, live, (((1,), (1,)), ((), ())), preferred_element_type=jnp.float32
    ).astype(jnp.bfloat16)
    cells = jnp.dot(by_row, spread.astype(jnp.bfloat16), preferred_element_type=jnp.float32)
    position = holder * kv_dev + lax.broadcasted_iota(jnp.int32, (1, kv_dev), 1)
    row1 = lax.broadcasted_iota(jnp.int32, (rows, 1), 0)
    at = offset + ((row1 // tile) ^ me) * q_dev + row1 % q_dev
    allowed = (position <= at) & ((position >= offset) | (cells > 0.5))
    return jnp.where(allowed, 0.0, MASKED)


def kernel(
    n, q_dev, offset_ref, live_hbm, q_hbm, k_hbm, v_hbm, out_ref,
    q_ref, live_ref, qbuf, kbuf, vbuf, lbuf, bias, obuf, rbuf, sbuf, sgot, diag,
    kv_sem, in_sem, l_send, l_recv, k_send, k_recv, v_send, v_recv,
    q_send, q_recv, o_send, o_recv, s_send, s_recv,
):
    me = lax.axis_index("kv")
    heads, tile, _ = q_hbm.shape
    kv_dev = k_hbm.shape[0]
    half = heads // 2
    per = half // CHUNKS
    wide = per * HD
    rows = n * tile
    far = n // 4
    core = me % 2
    y = me // 2 % 2
    z = me // 4
    mate = 1 - core

    def remote(src, dst, send, recv, slot):
        return pltpu.make_async_remote_copy(
            src_ref=src, dst_ref=dst, send_sem=send, recv_sem=recv,
            device_id={"kv": flip(me, slot)}, device_id_type=MESH,
        )

    def targets(step):
        found = []
        for k in range(1, far):
            if step > 0:
                to = k - 1 + (k - 1 + far - z) // far
            else:
                to = (z + far - k) % far
            base = xor(z, to, far) * 4
            for yd in range(2)[::step]:
                for cd in range(2):
                    slot = base + (y + yd) % 2 * 2 + (core + cd) % 2
                    found.append((slot, to * 4 + yd * 2 + cd, cd))
        for s in (3, 2, 1):
            found.append((s, flip(me, s), core if s % 2 == 0 else mate))
        return found

    def push(src, dst, send, recv, device):
        pltpu.make_async_remote_copy(
            src_ref=src, dst_ref=dst, send_sem=send, recv_sem=recv,
            device_id={"kv": device}, device_id_type=MESH,
        ).start()

    def columns(side, c):
        return pl.ds(pl.multiple_of(side * (half * HD) + c * wide, HD), wide)

    barrier = pltpu.get_barrier_semaphore()
    for s in reversed(range(1, n)):
        pl.semaphore_signal(
            barrier, inc=1, device_id={"kv": flip(me, s)}, device_id_type=MESH
        )
    q_load = pltpu.make_async_copy(q_hbm, q_ref, in_sem.at[0])
    live_load = pltpu.make_async_copy(live_hbm, live_ref, in_sem.at[1])
    q_load.start()
    live_load.start()
    own = pl.ds(0, kv_dev)
    theirs = pl.ds(kv_dev, kv_dev)
    loads = []
    for c in range(CHUNKS):
        here = pl.ds(c * wide, wide)
        k_load = pltpu.make_async_copy(
            k_hbm.at[:, columns(core, c)], kbuf.at[own, here], kv_sem.at[0, c]
        )
        v_load = pltpu.make_async_copy(
            v_hbm.at[:, columns(core, c)], vbuf.at[own, here], kv_sem.at[1, c]
        )
        k_load.start()
        v_load.start()
        loads.append((k_load, v_load))
    q_load.wait()
    pl.semaphore_wait(barrier, n - 1)

    live_copy = remote(live_hbm, lbuf, l_send.at[0], l_recv.at[0], 1)
    swaps = []
    outward = targets(-1)
    for c in range(CHUNKS):
        part = pl.ds(c * per, per)
        for slot, device, side in outward:
            push(
                q_ref.at[pl.ds(side * half + c * per, per)], qbuf.at[part, slot],
                q_send.at[c], q_recv.at[c], device,
            )
    live_copy.start()
    for c in range(CHUNKS):
        here = pl.ds(c * wide, wide)
        k_swap = remote(
            k_hbm.at[:, columns(mate, c)], kbuf.at[theirs, here], k_send.at[c], k_recv.at[c], 1
        )
        v_swap = remote(
            v_hbm.at[:, columns(mate, c)], vbuf.at[theirs, here], v_send.at[c], v_recv.at[c], 1
        )
        k_swap.start()
        v_swap.start()
        swaps.append((k_swap, v_swap))

    live_load.wait()
    qbuf[:, 0] = q_ref[pl.ds(core * half, half)]
    offset = offset_ref[0]
    bias[:, :kv_dev] = build_bias(n, tile, q_dev, me, me, kv_dev, live_ref, offset)
    live_copy.wait()
    bias[:, kv_dev:] = build_bias(n, tile, q_dev, me, flip(me, 1), kv_dev, lbuf, offset)

    inward = targets(1)
    others = pl.ds(1, n - 1)
    score_scale = LOG2E / math.sqrt(HD)
    strip = rows // SPLIT
    lane = lax.broadcasted_iota(jnp.int32, (strip, HD), 1)
    row = lax.broadcasted_iota(jnp.int32, (strip, HD), 0) % tile

    for c in range(CHUNKS):
        part = pl.ds(c * per, per)
        for copy in loads[c]:
            copy.wait()
        for copy in swaps[c]:
            copy.wait_recv()
        rest = qbuf.at[part, others]
        pltpu.make_async_copy(rest, rest, q_recv.at[c]).wait()
        for g in range(c * per, (c + 1) * per):
            cols = slice(g * HD, (g + 1) * HD)
            for r in range(SPLIT):
                mine = slice(r * strip, (r + 1) * strip)
                slots = slice(r * n // SPLIT, (r + 1) * n // SPLIT)
                queries = qbuf[g, slots].reshape(strip, HD)
                accs, peaks, totals = [], [], []
                for seg in range(2 * kv_dev // SEG):
                    keys = slice(seg * SEG, (seg + 1) * SEG)
                    scores = lax.dot_general(
                        queries, kbuf[keys, cols], (((1,), (1,)), ((), ())),
                        preferred_element_type=jnp.float32,
                    )
                    scores = scores * score_scale + bias[mine, keys]
                    peak = jnp.max(scores, axis=1, keepdims=True)
                    peak = jnp.maximum(peak, SCORE_FLOOR * LOG2E)
                    weights = jnp.exp2(scores - peak)
                    totals.append(jnp.sum(weights, axis=1, keepdims=True))
                    peaks.append(peak)
                    accs.append(
                        jnp.dot(
                            weights.astype(jnp.bfloat16), vbuf[keys, cols],
                            preferred_element_type=jnp.float32,
                        )
                    )
                peak = functools.reduce(jnp.maximum, peaks)
                scales = [jnp.exp2(p - peak) for p in peaks]
                acc = sum(a * e for a, e in zip(accs, scales))
                total = sum(t * e for t, e in zip(totals, scales))
                most = jnp.max(jnp.abs(acc), axis=1, keepdims=True)
                inverse = jnp.where(most > 0.0, STEPS / most, 0.0)
                coded = jnp.round(acc * inverse).astype(jnp.int32).astype(jnp.int16)
                obuf[g, slots] = coded.reshape(n // SPLIT, tile, HD)
                some = total > 0.0
                level = jnp.where(some, peak + jnp.log2(total), MASKED)
                ratio = jnp.where(some, most / total, 0.0)
                before = 0.0 if g == 0 else diag[mine]
                here = lane == g * tile + row
                there = lane == HD // 2 + g * tile + row
                diag[mine] = jnp.where(here, level, jnp.where(there, ratio, before))
        if c == CHUNKS - 1:
            for s in range(n):
                line = jnp.sum(diag[s * tile : (s + 1) * tile], axis=0, keepdims=True)
                if s == 0:
                    sgot[0, 0] = line
                else:
                    sbuf[s] = line
        for slot, device, _ in inward:
            if c == CHUNKS - 1:
                push(
                    sbuf.at[slot], sgot.at[slot // 2, slot % 2], s_send.at[0], s_recv.at[0], device
                )
            push(obuf.at[part, slot], rbuf.at[part, slot], o_send.at[c], o_recv.at[c], device)

    stats_in = sbuf.at[others]
    pltpu.make_async_copy(stats_in, stats_in, s_recv.at[0]).wait()
    weight = []
    for a in range(2):
        levels = sgot[:, a, 0]
        ratios = pltpu.roll(levels, HD // 2, 1)
        scale = jnp.exp2(levels - jnp.max(levels, axis=0, keepdims=True))
        total = jnp.sum(scale, axis=0, keepdims=True)
        weight.append(jnp.transpose(scale * (ratios / total)))
    for c in range(CHUNKS):
        part = pl.ds(c * per, per)
        rest = rbuf.at[part, others]
        pltpu.make_async_copy(rest, rest, o_recv.at[c]).wait()
        for g in range(c * per, (c + 1) * per):
            span = slice(g * tile, (g + 1) * tile)
            for a in range(2):
                acc = None
                for chip in range(n // 2):
                    s = chip * 2 + a
                    block = obuf[g, 0] if s == 0 else rbuf[g, s]
                    term = block.astype(jnp.int32).astype(jnp.float32)
                    term = term * weight[a][span, chip : chip + 1]
                    acc = term if acc is None else acc + term
                side = core if a == 0 else mate
                out_ref[side * half + g] = (acc * (1.0 / STEPS)).astype(jnp.bfloat16)

    for c in range(CHUNKS):
        part = pl.ds(c * per, per)
        rest = qbuf.at[part, others]
        pltpu.make_async_copy(rest, rest, q_send.at[c]).wait()
        for copy in swaps[c]:
            copy.wait_send()
        rest = obuf.at[part, others]
        pltpu.make_async_copy(rest, rest, o_send.at[c]).wait()
    pltpu.make_async_copy(stats_in, stats_in, s_send.at[0]).wait()


def on_device(queries, keys, values, block_live, span_offset):
    n = lax.axis_size("kv")
    q_dev, width = queries.shape
    kv_dev, kv_width = keys.shape
    shards, blocks = block_live.shape
    heads = kv_width // HD
    half = heads // 2
    group = width // kv_width
    tile = group * q_dev
    rows = n * tile
    assert half * tile <= HD // 2
    tiles = queries.reshape(q_dev, heads * group, HD).transpose(1, 0, 2).reshape(heads, tile, HD)
    vmem = pl.BlockSpec(memory_space=pltpu.VMEM)
    hbm = pl.BlockSpec(memory_space=pltpu.HBM)
    dma = pltpu.SemaphoreType.DMA
    out = pl.pallas_call(
        functools.partial(kernel, n, q_dev),
        out_shape=jax.ShapeDtypeStruct((heads, tile, HD), jnp.bfloat16),
        in_specs=[pl.BlockSpec(memory_space=pltpu.SMEM), hbm, hbm, hbm, hbm],
        out_specs=vmem,
        scratch_shapes=[
            pltpu.VMEM((heads, tile, HD), jnp.bfloat16),
            pltpu.VMEM((blocks, shards), jnp.int32),
            pltpu.VMEM((half, n, tile, HD), jnp.bfloat16),
            pltpu.VMEM((2 * kv_dev, kv_width // 2), jnp.bfloat16),
            pltpu.VMEM((2 * kv_dev, kv_width // 2), jnp.bfloat16),
            pltpu.VMEM((blocks, shards), jnp.int32),
            pltpu.VMEM((rows, 2 * kv_dev), jnp.float32),
            pltpu.VMEM((half, n, tile, HD), jnp.int16),
            pltpu.VMEM((half, n, tile, HD), jnp.int16),
            pltpu.VMEM((n, 1, HD), jnp.float32),
            pltpu.VMEM((n // 2, 2, 1, HD), jnp.float32),
            pltpu.VMEM((rows, HD), jnp.float32),
            dma((2, CHUNKS)), dma((2,)), dma((1,)), dma((1,)),
            *[dma((CHUNKS,)) for _ in range(8)],
            dma((1,)), dma((1,)),
        ],
        compiler_params=pltpu.CompilerParams(
            collective_id=0, has_side_effects=True, vmem_limit_bytes=53 * 1024 * 1024
        ),
    )(span_offset, *(pltpu.with_memory_space_constraint(x, pltpu.HBM) for x in (block_live.T, tiles, keys, values)))
    return out.reshape(heads * group, q_dev, HD).transpose(1, 0, 2).reshape(q_dev, width)


def solution(mesh):
    placed = (
        P(("groups", "kv"), None),
        P(("groups", "kv"), None),
        P(("groups", "kv"), None),
        P("groups", "kv"),
        P("groups"),
    )
    return jax.shard_map(
        on_device, mesh=mesh, in_specs=placed, out_specs=P(("groups", "kv"), None), check_vma=False
    )
```
